256 devices in a mesh: vec: 16 (over y, z_lo, core), state: 16 (over x, z_hi).
Axes of the slice: x: 4, y: 4, z: 8 (z_hi: 4, z_lo: 2; z = z_hi * 2 + z_lo), core: 2. Of those that a mesh axis runs over, the one named last changes fastest.
Arguments:
- beliefs: bfloat16 [2048, 32768], P('vec', 'state'), may hold values from 0.05 to 1
- tiles: bfloat16 [1024, 256, 256], P('state'), may hold values from 0 to 1
- tile_src: int32 [1024], P('state'), may hold values from 0 to 127, as said below
- tile_dst: int32 [1024], P('state'), may hold values from 0 to 127, as said below
- tile_action: int32 [1024], P('state'), may hold values from 0 to 7, as said below
- obs_prob: bfloat16 [8, 32, 32768], P(None, None, 'state'), may hold values from 0.049804688 to 1
- action_index: int32 [2048], P('vec'), may hold values from 0 to 7
- obs_index: int32 [2048], P('vec'), may hold values from 0 to 31
- alphas: bfloat16 [2048, 32768], P('vec', 'state'), may hold values from -1536 to 1536
Outputs:
- new_belief: bfloat16 [2048, 32768], P('vec', 'state')
- value: float32 [2048], P(('vec', 'state'))
The draws below stay inside these ranges and needn't reach their ends.
Inputs may be any that keep to these rules, and one draw needn't show every extreme that they name: `tile_dst`: the slots of index j of state, slots j * 64 to (j + 1) * 64 - 1, name destination tiles j * 8 to (j + 1) * 8 - 1. `tile_action`: each index of state holds exactly 8 slots of every action. `tile_src`: among the slots of any one action, every source tile is named exactly once.
All inputs are finite; a program needn't handle non-finite values.
Results may differ from the reference program's by a relative error of at most 0.0015.
Values may be sent and summed in bfloat16 or wider, within the bound.
A program may use at most 128 MiB of HBM per device.

```python
import math
import jax
import jax.numpy as jnp
from jax import lax

TILE = 256
ACT = 8
OBS = 32
TILES_DEV = 8
NT_DEV = 64
STATES = 32768
TILES = 128
NT = 1024
BELIEFS = 2048
ALPHAS = 2048
N_STATE = 16


def tile_layout(key):
    perm_keys = jax.random.split(jax.random.fold_in(key, 101), ACT)
    source_perms = jax.vmap(lambda k: jax.random.permutation(k, TILES))(perm_keys)
    source_perms = source_perms.astype(jnp.int32)
    by_device = source_perms.reshape(ACT, N_STATE, TILES_DEV)
    by_device = jnp.transpose(by_device, (1, 0, 2)).reshape(N_STATE, NT_DEV)
    action_grid = jnp.broadcast_to(jnp.arange(ACT, dtype=jnp.int32)[None, :, None], (N_STATE, ACT, TILES_DEV)).reshape(N_STATE, NT_DEV)
    order_keys = jax.random.split(jax.random.fold_in(key, 202), N_STATE)
    orders = jax.vmap(lambda k: jax.random.permutation(k, NT_DEV))(order_keys).astype(jnp.int32)
    sources = jnp.take_along_axis(by_device, orders, axis=1).reshape(NT)
    actions = jnp.take_along_axis(action_grid, orders, axis=1).reshape(NT)
    return (sources, actions)


def draw_tile_src(key, part):
    return tile_layout(key)[0]


def draw_tile_action(key, part):
    return tile_layout(key)[1]


def draw_tile_dst(key, part):
    slot_ids = jnp.arange(NT, dtype=jnp.int32)
    owner_ids = slot_ids // NT_DEV
    return owner_ids * TILES_DEV + jax.random.randint(jax.random.fold_in(key, 303), (NT,), 0, TILES_DEV, dtype=jnp.int32)


def draw_beliefs(key, part):
    keys = jax.random.split(jax.random.fold_in(key, 404), 5)
    blocks = STATES // TILE
    picked = jax.random.uniform(keys[0], (BELIEFS, blocks), jnp.float32) < 0.125
    high_level = jax.random.uniform(keys[1], (BELIEFS, blocks), jnp.float32, 0.7, 1.0)
    low_level = jax.random.uniform(keys[2], (BELIEFS, blocks), jnp.float32, 0.22, 0.3)
    level = jnp.where(picked, high_level, low_level)
    within = jax.random.uniform(keys[4], (BELIEFS, blocks, TILE), jnp.float32, 0.25, 1.0)
    return (level[:, :, None] * within).reshape(BELIEFS, STATES).astype(jnp.bfloat16)


def draw_tiles(key, part):
    keys = jax.random.split(jax.random.fold_in(key, 505), 4)
    level = jnp.exp(jax.random.uniform(keys[0], (NT, 1, 1), jnp.float32, -2.0, 0.0))
    row_scale = jnp.exp(jax.random.uniform(keys[2], (NT, TILE, 1), jnp.float32, -math.log(10.0), 0.0))
    entries = jax.random.uniform(keys[3], (NT, TILE, TILE), jnp.float32, 0.05, 1.0)
    return (level * row_scale * entries).astype(jnp.bfloat16)


def set_ends(values, stream_key, smallest, largest):
    place = [jax.random.randint(jax.random.fold_in(stream_key, axis), (), 0, length) for axis, length in enumerate(values.shape)]
    widest = values.shape.index(max(values.shape))
    beside = place[:widest] + [(place[widest] + 1) % values.shape[widest]] + place[widest + 1:]
    return values.at[tuple(place)].set(smallest).at[tuple(beside)].set(largest)


def steps_of(rng, shape, cuts, least, high):
    def one(axis_at, shards_of):
        draws = jax.random.uniform(jax.random.fold_in(jax.random.fold_in(rng, 6), axis_at), (shards_of,), jnp.float32, least / len(cuts), high / len(cuts))
        return jnp.repeat(jnp.exp(draws), shape[axis_at] // shards_of).reshape((-1,) + (1,) * (len(shape) - axis_at - 1))

    factor_of = one(*cuts[0])
    for cut in cuts[1:]:
        factor_of = factor_of * one(*cut)
    return factor_of


def centred(own_key, extent, width, bound, cuts=(), kind=jnp.bfloat16):
    gain = steps_of(own_key, extent, cuts, -0.22, 0.18) if cuts else 1.0
    values = jax.random.normal(own_key, extent, jnp.float32) * width * gain
    return jnp.minimum(jnp.maximum(values, -bound), bound).astype(kind)


def setup_inputs(seed: int = 0) -> dict:
    splits = jax.random.split(jax.random.key(seed), 10)
    return {
        "beliefs": draw_beliefs(jax.random.fold_in(splits[9], 71), 0),
        "tiles": draw_tiles(jax.random.fold_in(splits[9], 71), 0),
        "tile_src": draw_tile_src(jax.random.fold_in(splits[9], 71), 0),
        "tile_dst": draw_tile_dst(jax.random.fold_in(splits[9], 71), 0),
        "tile_action": draw_tile_action(jax.random.fold_in(splits[9], 71), 0),
        "obs_prob": jnp.clip(jnp.exp(math.log(1.0) - 2.9996462 * jax.random.uniform(splits[5], (ACT, OBS, STATES), jnp.float32) ** steps_of(splits[5], (ACT, OBS, STATES), ((2, 16),), -0.2, 0.2)), 0.049804688, 1.0).astype(jnp.bfloat16),
        "action_index": set_ends(jax.random.randint(splits[6], (BELIEFS,), 0, ACT), jax.random.fold_in(splits[6], 1), 0, ACT - 1).astype(jnp.int32),
        "obs_index": set_ends(jax.random.randint(splits[7], (BELIEFS,), 0, OBS), jax.random.fold_in(splits[7], 1), 0, OBS - 1).astype(jnp.int32),
        "alphas": centred(splits[8], (ALPHAS, STATES), 256.0, 1536.0, ((0, 16), (1, 16))),
    }


def reference(beliefs, tiles, tile_src, tile_dst, tile_action, obs_prob, action_index, obs_index, alphas):
    nbeliefs = beliefs.shape[0]

    def add_tile(running, tile_items):
        tile_vals, src_id, dst_id, act_id = tile_items
        columns = lax.dynamic_slice_in_dim(beliefs, (src_id * TILE).astype(jnp.int32), TILE, 1)
        contrib = jnp.dot(columns, tile_vals, preferred_element_type=jnp.float32)
        contrib = contrib * (action_index == act_id).astype(jnp.float32)[:, None]
        start_col = (dst_id * TILE).astype(jnp.int32)
        current = lax.dynamic_slice_in_dim(running, start_col, TILE, 1)
        running = lax.dynamic_update_slice_in_dim(running, current + contrib, start_col, 1)
        return running, None

    reached, _ = lax.scan(add_tile, jnp.zeros((nbeliefs, STATES), jnp.float32), (tiles, tile_src, tile_dst, tile_action))
    obs_rows = obs_prob[action_index, obs_index].astype(jnp.float32)
    unnorm = reached * obs_rows
    totals = jnp.sum(unnorm, axis=1)
    new_belief = ((float(STATES) * unnorm) / totals[:, None]).astype(jnp.bfloat16)
    scores = jnp.dot(new_belief, alphas.T, preferred_element_type=jnp.float32)
    value = jnp.max(scores, axis=1) / float(STATES)
    return new_belief, value
```

```python
import functools

import jax
import jax.numpy as jnp
from jax import lax
from jax.experimental import pallas as pl
from jax.experimental.pallas import tpu as pltpu
from jax.sharding import PartitionSpec as P

TILE = 256
ACT = 8
OBS = 32
KS = 8
NX = 4
NZ = 4
PIECES = 4
MESH = pl.DeviceIdType.MESH
F32 = jnp.float32
BF16 = jnp.bfloat16


def remote(src, dst, send, recv, dev):
    return pltpu.make_async_remote_copy(
        src_ref=src, dst_ref=dst, send_sem=send, recv_sem=recv, device_id=dev, device_id_type=MESH
    )


def greet(devs):
    barrier = pltpu.get_barrier_semaphore()
    for dev in devs:
        pl.semaphore_signal(barrier, inc=1, device_id=dev, device_id_type=MESH)
    pl.semaphore_wait(barrier, len(devs))


def exchange_kernel(
    tab_ref, act_ref, bel_ref, alp_ref, out_ref, all_ref,
    g0_ref, g1_ref, g2_ref, g3_ref, pick_ref, land_ref, tabs_ref, smem_ref, mask_ref,
    bel_sem, loc_sem, tab_send, tab_recv, tab_loc, z_send, z_recv, f_send, f_recv, x_send, x_recv,
    b_send, b_recv,
):
    v = lax.axis_index("vec")
    s = lax.axis_index("state")
    x, zh = s // NZ, s % NZ
    y, zl, core = v // 4, (v // 2) % 2, v % 2
    rows = bel_ref.shape[0]
    rp = rows // PIECES

    def at_state(xx, zz):
        return (v, xx * NZ + zz)

    def at_vec(yy, ll, cc):
        return (yy * 4 + ll * 2 + cc, s)

    z_dev = [at_state(x, (zh + 1) % NZ), at_state(x, (zh + 3) % NZ)]
    x_dev = [at_state((x + j) % NX, zh) for j in range(1, NX)]
    y_dev = [at_vec((y + 1) % 4, zl, core), at_vec((y + 3) % 4, zl, core)]
    pair_dev = at_vec(y, 1 - zl, core)
    sib_dev = at_vec(y, zl, 1 - core)

    g_refs = [g0_ref, g1_ref, g2_ref, g3_ref]
    own_bel = {}
    for p in range(PIECES):
        for t in range(KS):
            own_bel[p, t] = pltpu.make_async_copy(
                bel_ref.at[pl.ds(p * rp, rp), pl.ds(t * TILE, TILE)],
                g_refs[p].at[zh * KS + t], bel_sem.at[p, t],
            )
            own_bel[p, t].start()
    own_tab = pltpu.make_async_copy(tab_ref, smem_ref.at[0], loc_sem.at[2])
    own_tab.start()
    own_alp = pltpu.make_async_copy(alp_ref, all_ref.at[v], loc_sem.at[1])
    own_alp.start()
    greet(z_dev + x_dev + y_dev + [pair_dev, sib_dev])
    for c in own_bel.values():
        c.wait()

    tab_copies = []
    for j in range(1, NX):
        c = remote(tab_ref, tabs_ref.at[j], tab_send.at[j], tab_recv.at[j], x_dev[j - 1])
        c.start()
        tab_copies.append(c)

    def own_send(p, d):
        part = g_refs[p].at[pl.ds(zh * KS, KS)]
        return remote(part, part, z_send.at[d, p], z_recv.at[d, p], z_dev[d])

    def forward(p, d):
        origin = (zh + 3) % NZ if d == 0 else (zh + 1) % NZ
        part = g_refs[p].at[pl.ds(origin * KS, KS)]
        return remote(part, part, f_send.at[p], f_recv.at[p], z_dev[d])

    sends = []

    def go(c):
        c.start()
        sends.append(c)
        return c

    own = {}
    for p in range(2):
        for d in range(2):
            own[p, d] = go(own_send(p, d))

    n_b = [0]

    def b_copy(src, dst, dev):
        i = n_b[0]
        n_b[0] += 1
        return go(remote(src, dst, b_send.at[i], b_recv.at[i], dev))

    half = rows // 2

    def block(yy, ll, lo=0, n=rows):
        return all_ref.at[yy * 4 + ll * 2 + core, pl.ds(lo, n)]

    mine = all_ref.at[v]
    b_up = b_copy(alp_ref, mine, y_dev[0])
    b_down = b_copy(alp_ref, mine, y_dev[1])
    b_pair = b_copy(alp_ref, mine, pair_dev)
    b_sib = [b_copy(alp_ref, mine, sib_dev)]
    stage = {}

    def ring_forward(name, ll, up, down):
        up.wait_recv()
        lo = block((y + 3) % 4, ll, 0, half)
        stage[name, 0] = b_copy(lo, lo, y_dev[0])
        down.wait_recv()
        hi = block((y + 1) % 4, ll, half, half)
        stage[name, 1] = b_copy(hi, hi, y_dev[1])
        for yy in ((y + 3) % 4, (y + 1) % 4):
            whole = block(yy, ll)
            b_sib.append(b_copy(whole, whole, sib_dev))

    def ring_end(name, ll):
        stage[name, 0].wait_recv()
        stage[name, 1].wait_recv()
        whole = block((y + 2) % 4, ll)
        b_sib.append(b_copy(whole, whole, sib_dev))

    mask_ref[...] = jnp.zeros_like(mask_ref)
    for a in range(ACT):
        hit = jnp.where(act_ref[...] == a, 1.0, 0.0).astype(F32)
        hit = jnp.broadcast_to(hit, (rows, TILE)).astype(BF16)
        for p in range(PIECES):
            mask_ref[(p * ACT + a) * NX] = hit[p * rp : (p + 1) * rp]

    for c in tab_copies:
        c.wait()
    to_smem = pltpu.make_async_copy(tabs_ref.at[pl.ds(1, NX - 1)], smem_ref.at[pl.ds(1, NX - 1)], tab_loc)
    to_smem.start()
    to_smem.wait()
    own_tab.wait()

    def pick(j, p, into):
        def one(k, carry):
            acc = None
            for a in range(ACT):
                src = smem_ref[(NX - j) % NX, 0, a * KS + k]
                tile = g_refs[p][src & (NZ * KS - 1)]
                away = ((src >> 5) + NX - x) & (NX - 1)
                m = mask_ref[(p * ACT + a) * NX + away]
                acc = tile * m if acc is None else acc + tile * m
            into[k, pl.ds(p * rp, rp)] = acc
            return carry

        lax.fori_loop(0, KS, one, 0)

    fwd = {}
    x_copies = []
    partner = 1 - zl
    later = {}
    for p in range(PIECES):
        own[p, 0].wait_recv()
        if p % 2 == 0:
            fwd[p] = go(forward(p, 0))
        own[p, 1].wait_recv()
        if p % 2 == 1:
            fwd[p] = go(forward(p, 1))
        if p + 2 < PIECES:
            for d in range(2):
                own[p + 2, d] = go(own_send(p + 2, d))
        if p == 0:
            ring_forward(0, zl, b_up, b_down)
        if p == 1:
            ring_end(0, zl)
            b_pair.wait_recv()
            whole = block(y, partner)
            later[0] = b_copy(whole, whole, y_dev[0])
            later[1] = b_copy(whole, whole, y_dev[1])
            b_sib.append(b_copy(whole, whole, sib_dev))
        if p == 2:
            ring_forward(1, partner, later[0], later[1])
        fwd[p].wait_recv()
        for j in range(1, NX):
            pick(j, p, pick_ref.at[j])
            part = pl.ds(p * rp, rp)
            x_copies.append(
                go(remote(
                    pick_ref.at[j, :, part], land_ref.at[j, :, part],
                    x_send.at[j, p], x_recv.at[j, p], x_dev[j - 1],
                ))
            )
        pick(0, p, land_ref.at[0])
    ring_end(1, partner)

    for c in x_copies:
        c.wait_recv()

    def merge(k, carry):
        out_ref[k] = (land_ref[0, k] + land_ref[1, k]) + (land_ref[2, k] + land_ref[3, k])
        return carry

    lax.fori_loop(0, KS, merge, 0)
    own_alp.wait()
    for c in b_sib:
        c.wait_recv()
    for c in sends:
        c.wait_send()


def exchange(tab, act, beliefs, alphas, n_vec):
    rows, cols = beliefs.shape
    dma = pltpu.SemaphoreType.DMA
    vmem = pl.BlockSpec(memory_space=pltpu.VMEM)
    return pl.pallas_call(
        exchange_kernel,
        out_shape=(
            jax.ShapeDtypeStruct((KS, rows, TILE), BF16),
            jax.ShapeDtypeStruct((n_vec, rows, cols), BF16),
        ),
        in_specs=[vmem, vmem, pl.BlockSpec(memory_space=pl.ANY), vmem],
        out_specs=(vmem, pl.BlockSpec(memory_space=pl.ANY)),
        scratch_shapes=[
            *[pltpu.VMEM((NZ * KS, rows // PIECES, TILE), BF16)] * PIECES,
            pltpu.VMEM((NX, KS, rows, TILE), BF16),
            pltpu.VMEM((NX, KS, rows, TILE), BF16),
            pltpu.VMEM((NX, 8, 128), jnp.int32),
            pltpu.SMEM((NX, 8, 128), jnp.int32),
            pltpu.VMEM((PIECES * ACT * NX, rows // PIECES, TILE), BF16),
            dma((PIECES, KS)), dma((3,)), dma((NX,)), dma((NX,)), dma(()),
            dma((2, PIECES)), dma((2, PIECES)), dma((PIECES,)), dma((PIECES,)),
            dma((NX, PIECES)), dma((NX, PIECES)), dma((20,)), dma((20,)),
        ],
        compiler_params=pltpu.CompilerParams(
            collective_id=0, has_side_effects=True, vmem_limit_bytes=40 << 20
        ),
    )(tab, act, beliefs, alphas)


def tiles_kernel(
    sact_ref, rank_ref, dst_ref, act_ref, code_ref, src_ref, tiles_ref, obs_ref,
    unnorm_ref, u_ref, tot_ref, acc_ref, mask_ref,
):
    step = pl.program_id(0)
    per = tiles_ref.shape[0]
    rows = src_ref.shape[1]

    @pl.when(step == 0)
    def _():
        acc_ref[...] = jnp.zeros_like(acc_ref)
        for a in range(ACT):
            hit = jnp.where(act_ref[...] == a, 1.0, 0.0).astype(F32)
            mask_ref[a] = jnp.broadcast_to(hit, (rows, TILE)).astype(BF16)

    for i in range(per):
        t = step * per + i
        left = src_ref[rank_ref[t]] * mask_ref[sact_ref[t]]
        part = jnp.dot(left, tiles_ref[i], preferred_element_type=F32)
        d = dst_ref[t]
        acc_ref[d] = acc_ref[d] + part

    @pl.when(step == pl.num_programs(0) - 1)
    def _():
        codes = lax.broadcasted_iota(jnp.int32, (rows, ACT * OBS), 1)
        hot = jnp.where(code_ref[...] == codes, 1.0, 0.0).astype(BF16)
        total = jnp.zeros((rows, 1), F32)
        for d in range(acc_ref.shape[0]):
            cols = pl.ds(d * TILE, TILE)
            seen = jnp.dot(hot, obs_ref[:, cols], preferred_element_type=F32)
            un = acc_ref[d] * seen
            unnorm_ref[:, cols] = un
            u_ref[:, cols] = un.astype(BF16)
            total = total + jnp.sum(un, axis=1, keepdims=True)
        tot_ref[...] = jnp.transpose(jnp.broadcast_to(total, (rows, rows)))[:8]


def tile_products(sact, rank, dst, act, code, src, tiles, obs):
    _, rows, _ = src.shape
    nt = tiles.shape[0]
    cols = obs.shape[1]
    per = 8
    whole = pl.BlockSpec(memory_space=pltpu.VMEM)
    return pl.pallas_call(
        tiles_kernel,
        out_shape=(
            jax.ShapeDtypeStruct((rows, cols), F32),
            jax.ShapeDtypeStruct((rows, cols), BF16),
            jax.ShapeDtypeStruct((8, rows), F32),
        ),
        grid_spec=pltpu.PrefetchScalarGridSpec(
            num_scalar_prefetch=3,
            grid=(nt // per,),
            in_specs=[whole, whole, whole, pl.BlockSpec((per, TILE, TILE), lambda i, *_: (i, 0, 0)), whole],
            out_specs=[whole, whole, whole],
            scratch_shapes=[
                pltpu.VMEM((cols // TILE, rows, TILE), F32),
                pltpu.VMEM((ACT, rows, TILE), BF16),
            ],
        ),
        compiler_params=pltpu.CompilerParams(vmem_limit_bytes=40 << 20),
    )(sact, rank, dst, act, code, src, tiles, obs)


NB = 8


def score_kernel(
    scale, unnorm_ref, u_ref, tot_ref, all_ref, new_ref, val_ref,
    b_ref, c_ref, xr_ref, d_ref, zr_ref, tots_ref, tcol_ref,
    ld_sem, t_send, t_recv, x_send, x_recv, z_send, z_recv,
):
    v = lax.axis_index("vec")
    s = lax.axis_index("state")
    x, zh = s // NZ, s % NZ
    rows = u_ref.shape[0]
    wide = b_ref.shape[1]
    n_state = NX * NZ

    loads = []
    for n in range(NB):
        c = pltpu.make_async_copy(all_ref.at[pl.ds(n * wide, wide)], b_ref.at[n], ld_sem.at[n])
        c.start()
        loads.append(c)

    peers = [(v, (s + i) % n_state) for i in range(1, n_state)]
    greet(peers)

    sends = []

    def go(c):
        c.start()
        sends.append(c)
        return c

    tot_copies = [
        go(remote(tot_ref, tots_ref.at[i], t_send.at[i], t_recv.at[i], peers[i - 1]))
        for i in range(1, n_state)
    ]
    tots_ref[0] = tot_ref[...]

    quarter = rows // NX
    x_copies = {}
    for n in range(NB):
        loads[n].wait()
        c_ref[n] = lax.dot_general(
            u_ref[...], b_ref[n], (((1,), (1,)), ((), ())), preferred_element_type=F32
        )
        for j in (2, 1, 3):
            xx = (x + j) % NX
            x_copies[n, j] = go(remote(
                c_ref.at[n, pl.ds(xx * quarter, quarter)], xr_ref.at[n, j],
                x_send.at[n, j], x_recv.at[n, j], (v, xx * NZ + zh),
            ))

    for c in tot_copies:
        c.wait_recv()
    total = jnp.zeros((8, rows), F32)
    for q in range(n_state):
        total = total + tots_ref[(s + n_state - q) % n_state]
    tcol_ref[...] = jnp.transpose(jnp.broadcast_to(total[0:1], (rows, rows)))

    def norm(i, carry):
        cols = pl.ds(pl.multiple_of(i * rows, rows), rows)
        new_ref[:, cols] = ((scale * unnorm_ref[:, cols]) / tcol_ref[...]).astype(BF16)
        return carry

    lax.fori_loop(0, unnorm_ref.shape[1] // rows, norm, 0)

    each = quarter // NZ
    z_copies = {}
    for h in range(2):
        for n in range(h * NB // 2, (h + 1) * NB // 2):
            for j in range(1, NX):
                x_copies[n, j].wait_recv()
            mine = c_ref[n, pl.ds(pl.multiple_of(x * quarter, quarter), quarter)]
            d_ref[n] = (mine + xr_ref[n, 1]) + (xr_ref[n, 2] + xr_ref[n, 3])
        part = pl.ds(h * NB // 2, NB // 2)
        for j in (2, 1, 3):
            zz = (zh + j) % NZ
            z_copies[h, j] = go(remote(
                d_ref.at[part, pl.ds(zz * each, each)], zr_ref.at[j, part],
                z_send.at[h, j], z_recv.at[h, j], (v, x * NZ + zz),
            ))
    best = None
    for h in range(2):
        for j in range(1, NZ):
            z_copies[h, j].wait_recv()
        for n in range(h * NB // 2, (h + 1) * NB // 2):
            mine = d_ref[n, pl.ds(pl.multiple_of(zh * each, each), each)]
            full = (mine + zr_ref[1, n]) + (zr_ref[2, n] + zr_ref[3, n])
            best = full if best is None else jnp.maximum(best, full)
    top = jnp.max(best, axis=1, keepdims=True)
    mine = tcol_ref[pl.ds(pl.multiple_of(s * each, each), each)]
    val_ref[...] = jnp.broadcast_to(top, mine.shape) / mine
    for c in sends:
        c.wait_send()


def scores(unnorm, u, tot, alphas_all, scale):
    rows, cols = u.shape
    n_alpha = alphas_all.shape[0]
    wide = n_alpha // NB
    quarter = rows // NX
    n_state = NX * NZ
    dma = pltpu.SemaphoreType.DMA
    vmem = pl.BlockSpec(memory_space=pltpu.VMEM)
    return pl.pallas_call(
        functools.partial(score_kernel, scale),
        out_shape=(
            jax.ShapeDtypeStruct((rows, cols), BF16),
            jax.ShapeDtypeStruct((rows // n_state, rows), F32),
        ),
        in_specs=[vmem, vmem, vmem, pl.BlockSpec(memory_space=pl.ANY)],
        out_specs=(vmem, vmem),
        scratch_shapes=[
            pltpu.VMEM((NB, wide, cols), BF16),
            pltpu.VMEM((NB, rows, wide), F32),
            pltpu.VMEM((NB, NX, quarter, wide), F32),
            pltpu.VMEM((NB, quarter, wide), F32),
            pltpu.VMEM((NZ, NB, quarter // NZ, wide), F32),
            pltpu.VMEM((n_state, 8, rows), F32),
            pltpu.VMEM((rows, rows), F32),
            dma((NB,)), dma((n_state,)), dma((n_state,)),
            dma((NB, NX)), dma((NB, NX)), dma((2, NZ)), dma((2, NZ)),
        ],
        compiler_params=pltpu.CompilerParams(
            collective_id=1, has_side_effects=True, vmem_limit_bytes=40 << 20
        ),
    )(unnorm, u, tot, alphas_all)


def per_device(
    beliefs, tiles, tile_src, tile_dst, tile_action, obs_prob, action_index, obs_index, alphas
):
    shard_id = lax.axis_index("state")
    n_vec = lax.axis_size("vec")
    n_state = lax.axis_size("state")
    rows, cols = beliefs.shape
    nt = tile_src.shape[0]
    slots = jnp.arange(nt, dtype=jnp.int32)
    earlier = (tile_action[None, :] == tile_action[:, None]) & (slots[None, :] < slots[:, None])
    rank = jnp.sum(earlier.astype(jnp.int32), axis=1)
    place = tile_action * KS + rank
    lanes = jnp.arange(128, dtype=jnp.int32)
    table = jnp.sum(jnp.where(place[:, None] == lanes[None, :], tile_src[:, None], 0), axis=0)
    table = jnp.broadcast_to(table[None, :], (8, 128)).astype(jnp.int32)
    act_col = action_index[:, None]
    code_col = (action_index * OBS + obs_index)[:, None]
    local_dst = tile_dst - shard_id * (cols // TILE)

    src, alphas_all = exchange(table, act_col, beliefs, alphas, n_vec)
    unnorm, u, tot = tile_products(
        tile_action, rank, local_dst, act_col, code_col, src, tiles, obs_prob.reshape(ACT * OBS, cols)
    )
    new_belief, value = scores(
        unnorm, u, tot, alphas_all.reshape(n_vec * rows, cols), float(cols * n_state)
    )
    return new_belief, value[:, 0]


def solution(mesh):
    placed = (
        P("vec", "state"),
        P("state", None, None),
        P("state"),
        P("state"),
        P("state"),
        P(None, None, "state"),
        P("vec"),
        P("vec"),
        P("vec", "state"),
    )
    return jax.shard_map(
        per_device,
        mesh=mesh,
        in_specs=placed,
        out_specs=(P("vec", "state"), P(("vec", "state"))),
        check_vma=False,
    )
```

```python
import functools

import jax
import jax.numpy as jnp
from jax import lax
from jax.experimental import pallas as pl
from jax.experimental.pallas import tpu as pltpu
from jax.sharding import PartitionSpec as P

TILE = 256
ACT = 8
OBS = 32
KS = 8
NX = 4
NZ = 4
PIECES = 4
MESH = pl.DeviceIdType.MESH
F32 = jnp.float32
BF16 = jnp.bfloat16


def remote(src, dst, send, recv, dev):
    return pltpu.make_async_remote_copy(
        src_ref=src, dst_ref=dst, send_sem=send, recv_sem=recv, device_id=dev, device_id_type=MESH
    )


def greet(devs):
    for dev in devs:
        pl.semaphore_signal(
            pltpu.get_barrier_semaphore(), inc=1, device_id=dev, device_id_type=MESH
        )


def all_here(devs):
    pl.semaphore_wait(pltpu.get_barrier_semaphore(), len(devs))


def exchange_kernel(
    tsrc_ref, tact_ref, act_ref, bel_ref, alp_ref, out_ref, all_ref,
    g0_ref, g1_ref, g2_ref, g3_ref, pick_ref, relay_ref, land_ref, tabs_ref, smem_ref, mask_ref,
    bel_sem, loc_sem, tab_send, tab_recv, z_send, z_recv, f_send, f_recv,
    r_send, r_recv, x_send, x_recv, b_send, b_recv,
):
    v = lax.axis_index("vec")
    s = lax.axis_index("state")
    x, zh = s // NZ, s % NZ
    y, zl, core = v // 4, (v // 2) % 2, v % 2
    rows = bel_ref.shape[0]
    rp = rows // PIECES
    kh = KS // 2

    def at_state(xx, zz):
        return (v, xx * NZ + zz)

    def at_vec(yy, ll, cc):
        return (yy * 4 + ll * 2 + cc, s)

    z_dev = [at_state(x, (zh + 1) % NZ), at_state(x, (zh + 3) % NZ)]
    x_dev = [at_state((x + j) % NX, zh) for j in range(1, NX)]
    y_dev = [at_vec((y + 1) % 4, zl, core), at_vec((y + 3) % 4, zl, core)]
    pair_dev = at_vec(y, 1 - zl, core)
    sib_dev = at_vec(y, zl, 1 - core)

    near = z_dev + x_dev + y_dev + [pair_dev, sib_dev]
    greet(near)
    g_refs = [g0_ref, g1_ref, g2_ref, g3_ref]
    own_bel = {}
    for p in range(PIECES):
        for t in range(KS):
            own_bel[p, t] = pltpu.make_async_copy(
                bel_ref.at[pl.ds(p * rp, rp), pl.ds(t * TILE, TILE)],
                g_refs[p].at[zh * KS + t], bel_sem.at[p, t],
            )
            own_bel[p, t].start()
    own_alp = pltpu.make_async_copy(alp_ref, all_ref.at[v], loc_sem.at[0])
    own_alp.start()

    nt = tact_ref.shape[1]
    act_l = jnp.broadcast_to(tact_ref[...].astype(F32), (nt, nt))
    act_s = jnp.transpose(act_l)
    src_s = jnp.transpose(jnp.broadcast_to(tsrc_ref[...].astype(F32), (nt, nt)))
    before = lax.broadcasted_iota(jnp.int32, (nt, nt), 1) < lax.broadcasted_iota(jnp.int32, (nt, nt), 0)
    rank = jnp.sum(jnp.where((act_l == act_s) & before, 1.0, 0.0), axis=1, keepdims=True)
    lane = lax.broadcasted_iota(jnp.int32, (nt, 128), 1).astype(F32)
    by_rank = jnp.where(rank == lane, 1.0, 0.0)
    by_act = jnp.where(act_s[:, :1] == lane, src_s[:, :1], 0.0)
    table = lax.dot_general(
        by_rank.astype(BF16), by_act.astype(BF16), (((0,), (0,)), ((), ())), preferred_element_type=F32
    )
    tabs_ref[0] = table[:KS].astype(jnp.int32)

    mask_ref[...] = jnp.zeros_like(mask_ref)
    act_col = jnp.transpose(jnp.broadcast_to(act_ref[...].astype(F32), (rows, rows)))
    for a in range(ACT):
        hit = jnp.where(act_col == float(a), 1.0, 0.0).astype(BF16)
        for p in range(PIECES):
            for c in range(TILE // rows):
                mask_ref[(p * ACT + a) * NX, :, c * rows : (c + 1) * rows] = hit[p * rp : (p + 1) * rp]

    all_here(near)
    for c in own_bel.values():
        c.wait()

    sends = []

    def go(c):
        c.start()
        sends.append(c)
        return c

    def own_send(p, d):
        part = g_refs[p].at[pl.ds(zh * KS, KS)]
        return remote(part, part, z_send.at[d, p], z_recv.at[d, p], z_dev[d])

    def forward(p, d):
        origin = (zh + 3) % NZ if d == 0 else (zh + 1) % NZ
        part = g_refs[p].at[pl.ds(origin * KS + d * kh, kh)]
        return remote(part, part, f_send.at[d, p], f_recv.at[d, p], z_dev[d])

    own = {}
    for p in range(2):
        for d in range(2):
            own[p, d] = go(own_send(p, d))

    tab_copies = [
        go(remote(tabs_ref.at[0], tabs_ref.at[j], tab_send.at[j], tab_recv.at[j], x_dev[j - 1]))
        for j in range(1, NX)
    ]

    n_b = [0]

    def b_copy(src, dst, dev):
        i = n_b[0]
        n_b[0] += 1
        return go(remote(src, dst, b_send.at[i], b_recv.at[i], dev))

    half = rows // 2

    def block(yy, ll, lo=0, n=rows):
        return all_ref.at[yy * 4 + ll * 2 + core, pl.ds(lo, n)]

    mine = all_ref.at[v]
    b_up = b_copy(alp_ref, mine, y_dev[0])
    b_down = b_copy(alp_ref, mine, y_dev[1])
    b_pair = b_copy(alp_ref, mine, pair_dev)
    b_sib = [b_copy(alp_ref, mine, sib_dev)]
    stage = {}

    def ring_forward(name, ll, up, down):
        up.wait_recv()
        lo = block((y + 3) % 4, ll, 0, half)
        stage[name, 0] = b_copy(lo, lo, y_dev[0])
        down.wait_recv()
        hi = block((y + 1) % 4, ll, half, half)
        stage[name, 1] = b_copy(hi, hi, y_dev[1])
        for yy in ((y + 3) % 4, (y + 1) % 4):
            whole = block(yy, ll)
            b_sib.append(b_copy(whole, whole, sib_dev))

    def ring_end(name, ll):
        stage[name, 0].wait_recv()
        stage[name, 1].wait_recv()
        whole = block((y + 2) % 4, ll)
        b_sib.append(b_copy(whole, whole, sib_dev))

    for c in tab_copies:
        c.wait_recv()
    to_smem = pltpu.make_async_copy(tabs_ref, smem_ref, loc_sem.at[1])
    to_smem.start()
    to_smem.wait()

    def pick(j, p, into):
        def one(k, carry):
            acc = None
            for a in range(ACT):
                src = smem_ref[(NX - j) % NX, k, a]
                tile = g_refs[p][src & (NZ * KS - 1)]
                away = ((src >> 5) + NX - x) & (NX - 1)
                m = mask_ref[(p * ACT + a) * NX + away]
                acc = tile * m if acc is None else acc + tile * m
            into[k, pl.ds(p * rp, rp)] = acc
            return carry

        lax.fori_loop(0, KS, one, 0)

    fwd = {}
    x_copies = []

    def along_x(p):
        part = pl.ds(p * rp, rp)
        fwd[p, 0].wait_recv()
        fwd[p, 1].wait_recv()
        pick(2, p, pick_ref.at[0])
        relays = []
        for d in range(2):
            relays.append(go(remote(
                pick_ref.at[0, pl.ds(d * kh, kh), part], relay_ref.at[d, :, part],
                r_send.at[d, p], r_recv.at[d, p], x_dev[2 * d],
            )))
        pick(1, p, pick_ref.at[1])
        pick(3, p, pick_ref.at[2])
        pick(0, p, land_ref.at[0])
        for d in range(2):
            relays[d].wait_recv()
            for k in range(kh):
                pick_ref[1 + d, d * kh + k, part] = pick_ref[1 + d, d * kh + k, part] + relay_ref[d, k, part]
            x_copies.append(go(remote(
                pick_ref.at[1 + d, :, part], land_ref.at[1 + d, :, part],
                x_send.at[d, p], x_recv.at[d, p], x_dev[2 * d],
            )))

    partner = 1 - zl
    later = {}
    for p in range(PIECES):
        for d in range(2):
            own[p, d].wait_recv()
            fwd[p, d] = go(forward(p, d))
        if p + 2 < PIECES:
            for d in range(2):
                own[p + 2, d] = go(own_send(p + 2, d))
        if p == 1:
            ring_forward(0, zl, b_up, b_down)
        if p == 2:
            b_pair.wait_recv()
            whole = block(y, partner)
            later[0] = b_copy(whole, whole, y_dev[0])
            later[1] = b_copy(whole, whole, y_dev[1])
            b_sib.append(b_copy(whole, whole, sib_dev))
            ring_end(0, zl)
        if p:
            along_x(p - 1)
    ring_forward(1, partner, later[0], later[1])
    along_x(PIECES - 1)

    for c in x_copies:
        c.wait_recv()

    def merge(k, carry):
        out_ref[k] = (land_ref[0, k] + land_ref[1, k]) + land_ref[2, k]
        return carry

    lax.fori_loop(0, KS, merge, 0)
    ring_end(1, partner)
    own_alp.wait()
    for c in b_sib:
        c.wait_recv()
    for c in sends:
        c.wait_send()


BIG = 62 << 20


def exchange(tsrc, tact, act, beliefs, alphas, n_vec):
    rows, cols = beliefs.shape
    dma = pltpu.SemaphoreType.DMA
    vmem = pl.BlockSpec(memory_space=pltpu.VMEM)
    hbm = pl.BlockSpec(memory_space=pl.ANY)
    return pl.pallas_call(
        exchange_kernel,
        out_shape=(
            jax.ShapeDtypeStruct((KS, rows, TILE), BF16),
            jax.ShapeDtypeStruct((n_vec, rows, cols), BF16),
        ),
        in_specs=[vmem, vmem, vmem, hbm, hbm],
        out_specs=(vmem, hbm),
        scratch_shapes=[
            *[pltpu.VMEM((NZ * KS, rows // PIECES, TILE), BF16)] * PIECES,
            pltpu.VMEM((3, KS, rows, TILE), BF16),
            pltpu.VMEM((2, KS // 2, rows, TILE), BF16),
            pltpu.VMEM((3, KS, rows, TILE), BF16),
            pltpu.VMEM((NX, 8, 128), jnp.int32),
            pltpu.SMEM((NX, 8, 128), jnp.int32),
            pltpu.VMEM((PIECES * ACT * NX, rows // PIECES, TILE), BF16),
            dma((PIECES, KS)), dma((2,)), dma((NX,)), dma((NX,)),
            dma((2, PIECES)), dma((2, PIECES)), dma((2, PIECES)), dma((2, PIECES)),
            dma((2, PIECES)), dma((2, PIECES)), dma((2, PIECES)), dma((2, PIECES)),
            dma((20,)), dma((20,)),
        ],
        compiler_params=pltpu.CompilerParams(
            collective_id=0, has_side_effects=True, vmem_limit_bytes=BIG
        ),
    )(tsrc, tact, act, beliefs, alphas)


def tiles_kernel(
    sact_ref, dst_ref, act_ref, seen_ref, src_ref, tiles_ref, obs_ref,
    unnorm_ref, u_ref, tot_ref, acc_ref, mask_ref, count_ref,
):
    step = pl.program_id(0)
    per = tiles_ref.shape[0]
    rows = src_ref.shape[1]

    @pl.when(step == 0)
    def _():
        acc_ref[...] = jnp.zeros_like(acc_ref)
        act_col = jnp.transpose(jnp.broadcast_to(act_ref[...].astype(F32), (rows, rows)))
        for a in range(ACT):
            hit = jnp.where(act_col == float(a), 1.0, 0.0).astype(BF16)
            count_ref[a] = 0
            for c in range(TILE // rows):
                mask_ref[a, :, c * rows : (c + 1) * rows] = hit

    for i in range(per):
        t = step * per + i
        a = sact_ref[t]
        k = count_ref[a]
        count_ref[a] = k + 1
        left = src_ref[k] * mask_ref[a]
        part = jnp.dot(left, tiles_ref[i], preferred_element_type=F32)
        d = lax.rem(dst_ref[t], acc_ref.shape[0])
        acc_ref[d] = acc_ref[d] + part

    @pl.when(step == pl.num_programs(0) - 1)
    def _():
        code = act_ref[...] * OBS + seen_ref[...]
        codes = lax.broadcasted_iota(jnp.int32, (ACT * OBS, rows), 0)
        hot = jnp.where(codes == code, 1.0, 0.0).astype(BF16)
        total = jnp.zeros((rows, 1), F32)
        for d in range(acc_ref.shape[0]):
            cols = pl.ds(d * TILE, TILE)
            seen = lax.dot_general(
                hot, obs_ref[:, cols], (((0,), (0,)), ((), ())), preferred_element_type=F32
            )
            un = acc_ref[d] * seen
            unnorm_ref[:, cols] = un
            u_ref[:, cols] = un.astype(BF16)
            total = total + jnp.sum(un, axis=1, keepdims=True)
        tot_ref[...] = jnp.transpose(jnp.broadcast_to(total, (rows, rows)))[:8]


def tile_products(sact, dst, act, seen, src, tiles, obs):
    _, rows, _ = src.shape
    nt = tiles.shape[0]
    cols = obs.shape[1]
    per = 8
    whole = pl.BlockSpec(memory_space=pltpu.VMEM)
    return pl.pallas_call(
        tiles_kernel,
        out_shape=(
            jax.ShapeDtypeStruct((rows, cols), F32),
            jax.ShapeDtypeStruct((rows, cols), BF16),
            jax.ShapeDtypeStruct((8, rows), F32),
        ),
        grid_spec=pltpu.PrefetchScalarGridSpec(
            num_scalar_prefetch=2,
            grid=(nt // per,),
            in_specs=[whole, whole, whole, pl.BlockSpec((per, TILE, TILE), lambda i, *_: (i, 0, 0)), whole],
            out_specs=[whole, whole, whole],
            scratch_shapes=[
                pltpu.VMEM((cols // TILE, rows, TILE), F32),
                pltpu.VMEM((ACT, rows, TILE), BF16),
                pltpu.SMEM((ACT,), jnp.int32),
            ],
        ),
        compiler_params=pltpu.CompilerParams(vmem_limit_bytes=BIG),
    )(sact, dst, act, seen, src, tiles, obs)


NB = 8
GROUPS = 4


def score_kernel(
    scale, unnorm_ref, u_ref, tot_ref, all_ref, new_ref, val_ref,
    b_ref, c_ref, relay_ref, xr_ref, d_ref, zr_ref, tots_ref, tcol_ref,
    ld_sem, t_send, t_recv, r_send, r_recv, x_send, x_recv, z_send, z_recv,
):
    v = lax.axis_index("vec")
    s = lax.axis_index("state")
    x, zh = s // NZ, s % NZ
    rows = u_ref.shape[0]
    wide = b_ref.shape[1]
    n_state = NX * NZ

    loads = []
    for n in range(NB):
        c = pltpu.make_async_copy(all_ref.at[pl.ds(n * wide, wide)], b_ref.at[n], ld_sem.at[n])
        c.start()
        loads.append(c)

    peers = [(v, (s + i) % n_state) for i in range(1, n_state)]
    greet(peers)
    all_here(peers)

    sends = []

    def go(c):
        c.start()
        sends.append(c)
        return c

    tot_copies = [
        go(remote(tot_ref, tots_ref.at[i], t_send.at[i], t_recv.at[i], peers[i - 1]))
        for i in range(1, n_state)
    ]
    tots_ref[0] = tot_ref[...]

    quarter = rows // NX
    half = quarter // 2
    relays = {}
    x_copies = {}
    x_dev = [(v, (x + 1) % NX * NZ + zh), (v, (x + 3) % NX * NZ + zh)]

    def rows_of(j, lo=0, size=quarter):
        return pl.ds(pl.multiple_of((x + j) % NX * quarter + lo, half), size)

    def along_x(n):
        for d in range(2):
            relays[n, d].wait_recv()
            part = rows_of(1 + 2 * d, d * half, half)
            c_ref[n, part] = c_ref[n, part] + relay_ref[d, n]
            x_copies[n, d] = go(remote(
                c_ref.at[n, rows_of(1 + 2 * d)], xr_ref.at[d, n],
                x_send.at[n, d], x_recv.at[n, d], x_dev[d],
            ))

    for n in range(NB):
        loads[n].wait()
        c_ref[n] = lax.dot_general(
            u_ref[...], b_ref[n], (((1,), (1,)), ((), ())), preferred_element_type=F32
        )
        for d in range(2):
            relays[n, d] = go(remote(
                c_ref.at[n, rows_of(2, d * half, half)], relay_ref.at[d, n],
                r_send.at[n, d], r_recv.at[n, d], x_dev[d],
            ))
        if n:
            along_x(n - 1)
    along_x(NB - 1)

    each = quarter // NZ
    per = NB // GROUPS
    z_copies = {}
    for h in range(GROUPS):
        for n in range(h * per, (h + 1) * per):
            for d in range(2):
                x_copies[n, d].wait_recv()
            d_ref[n] = (c_ref[n, rows_of(0)] + xr_ref[0, n]) + xr_ref[1, n]
        part = pl.ds(h * per, per)
        for j in (2, 1, 3):
            zz = (zh + j) % NZ
            z_copies[h, j] = go(remote(
                d_ref.at[part, pl.ds(zz * each, each)], zr_ref.at[j, part],
                z_send.at[h, j], z_recv.at[h, j], (v, x * NZ + zz),
            ))

    for c in tot_copies:
        c.wait_recv()
    total = jnp.zeros((8, rows), F32)
    for q in range(n_state):
        total = total + tots_ref[(s + n_state - q) % n_state]
    tcol_ref[...] = jnp.transpose(jnp.broadcast_to(total[0:1], (rows, rows)))

    def norm(i, carry):
        cols = pl.ds(pl.multiple_of(i * rows, rows), rows)
        new_ref[:, cols] = ((scale * unnorm_ref[:, cols]) / tcol_ref[...]).astype(BF16)
        return carry

    lax.fori_loop(0, unnorm_ref.shape[1] // rows, norm, 0)

    best = None
    for h in range(GROUPS):
        for j in range(1, NZ):
            z_copies[h, j].wait_recv()
        for n in range(h * per, (h + 1) * per):
            mine = d_ref[n, pl.ds(pl.multiple_of(zh * each, each), each)]
            full = (mine + zr_ref[1, n]) + (zr_ref[2, n] + zr_ref[3, n])
            best = full if best is None else jnp.maximum(best, full)
    top = jnp.max(best, axis=1, keepdims=True)
    mine = tcol_ref[pl.ds(pl.multiple_of(s * each, each), each)]
    val_ref[...] = jnp.broadcast_to(top, mine.shape) / mine
    for c in sends:
        c.wait_send()


def scores(unnorm, u, tot, alphas_all, scale):
    rows, cols = u.shape
    n_alpha = alphas_all.shape[0]
    wide = n_alpha // NB
    quarter = rows // NX
    n_state = NX * NZ
    dma = pltpu.SemaphoreType.DMA
    vmem = pl.BlockSpec(memory_space=pltpu.VMEM)
    return pl.pallas_call(
        functools.partial(score_kernel, scale),
        out_shape=(
            jax.ShapeDtypeStruct((rows, cols), BF16),
            jax.ShapeDtypeStruct((rows // n_state, rows), F32),
        ),
        in_specs=[vmem, vmem, vmem, pl.BlockSpec(memory_space=pl.ANY)],
        out_specs=(vmem, vmem),
        scratch_shapes=[
            pltpu.VMEM((NB, wide, cols), BF16),
            pltpu.VMEM((NB, rows, wide), F32),
            pltpu.VMEM((2, NB, quarter // 2, wide), F32),
            pltpu.VMEM((2, NB, quarter, wide), F32),
            pltpu.VMEM((NB, quarter, wide), F32),
            pltpu.VMEM((NZ, NB, quarter // NZ, wide), F32),
            pltpu.VMEM((n_state, 8, rows), F32),
            pltpu.VMEM((rows, rows), F32),
            dma((NB,)), dma((n_state,)), dma((n_state,)),
            dma((NB, 2)), dma((NB, 2)), dma((NB, 2)), dma((NB, 2)), dma((GROUPS, NZ)), dma((GROUPS, NZ)),
        ],
        compiler_params=pltpu.CompilerParams(
            collective_id=1, has_side_effects=True, vmem_limit_bytes=BIG
        ),
    )(unnorm, u, tot, alphas_all)


def per_device(
    beliefs, tiles, tile_src, tile_dst, tile_action, obs_prob, action_index, obs_index, alphas
):
    n_vec = lax.axis_size("vec")
    n_state = lax.axis_size("state")
    rows, cols = beliefs.shape
    act_row = action_index[None, :]
    src, alphas_all = exchange(tile_src[None, :], tile_action[None, :], act_row, beliefs, alphas, n_vec)
    unnorm, u, tot = tile_products(
        tile_action, tile_dst, act_row, obs_index[None, :], src, tiles, obs_prob.reshape(ACT * OBS, cols)
    )
    new_belief, value = scores(
        unnorm, u, tot, alphas_all.reshape(n_vec * rows, cols), float(cols * n_state)
    )
    return new_belief, value[:, 0]


def solution(mesh):
    placed = (
        P("vec", "state"),
        P("state", None, None),
        P("state"),
        P("state"),
        P("state"),
        P(None, None, "state"),
        P("vec"),
        P("vec"),
        P("vec", "state"),
    )
    return jax.shard_map(
        per_device,
        mesh=mesh,
        in_specs=placed,
        out_specs=(P("vec", "state"), P(("vec", "state"))),
        check_vma=False,
    )
```

```python
import functools

import jax
import jax.numpy as jnp
from jax import lax
from jax.experimental import pallas as pl
from jax.experimental.pallas import tpu as pltpu
from jax.sharding import PartitionSpec as P

TILE = 256
ACT = 8
OBS = 32
KS = 8
NX = 4
NZ = 4
PIECE_ROWS = (32, 32, 32, 16, 16)
NB = 8
GROUPS = 4
BIG = 62 << 20
MESH = pl.DeviceIdType.MESH
F32 = jnp.float32
BF16 = jnp.bfloat16


def remote(src, dst, send, recv, dev):
    return pltpu.make_async_remote_copy(
        src_ref=src, dst_ref=dst, send_sem=send, recv_sem=recv, device_id=dev, device_id_type=MESH
    )


def greet(devs):
    for dev in devs:
        pl.semaphore_signal(
            pltpu.get_barrier_semaphore(), inc=1, device_id=dev, device_id_type=MESH
        )


def all_here(devs):
    pl.semaphore_wait(pltpu.get_barrier_semaphore(), len(devs))


def expand_kernel(
    scale, tsrc_ref, tact_ref, tdst_ref, act_ref, seen_ref, bel_ref, alp_ref, tiles_hbm, obs_hbm,
    new_ref, val_ref, *scratch,
):
    scratch = list(scratch)
    n_p = len(PIECE_ROWS)
    g_refs, scratch = scratch[:n_p], scratch[n_p:]
    m_refs, scratch = scratch[:n_p], scratch[n_p:]
    (
        pick_ref, land_ref, r_ref, full_ref, tabs_ref, slot_ref, smem_ref, slot_smem,
        tiles_ref, obs_ref, seg_ref, unnorm_ref, u_ref, b_ref, c_ref, xr_ref, d_ref, zr_ref,
        tot_ref, totx_ref, totz_ref, tcol_ref,
        bel_sem, loc_sem, tab_send, tab_recv, z_send, z_recv, f_send, f_recv, x_send, x_recv,
        b_send, b_recv, cx_send, cx_recv, cz_send, cz_recv, t_send, t_recv,
    ) = scratch
    v = lax.axis_index("vec")
    s = lax.axis_index("state")
    x, zh = s // NZ, s % NZ
    y, zl, core = v // 4, (v // 2) % 2, v % 2
    rows, cols = bel_ref.shape
    kh = KS // 2
    starts = [sum(PIECE_ROWS[:p]) for p in range(n_p)]

    def at_vec(yy, ll, cc):
        return (yy * 4 + ll * 2 + cc, s)

    x_dev = [(v, (x + j) % NX * NZ + zh) for j in range(1, NX)]
    z_all = [(v, x * NZ + (zh + j) % NZ) for j in range(1, NZ)]
    z_dev = [z_all[0], z_all[2]]
    y_dev = [at_vec((y + 1) % 4, zl, core), at_vec((y + 3) % 4, zl, core)]
    pair_dev = at_vec(y, 1 - zl, core)
    sib_dev = at_vec(y, zl, 1 - core)
    near = x_dev + z_all + y_dev + [pair_dev, sib_dev]
    greet(near)

    def block(yy, ll, lo=0, n=rows):
        return b_ref.at[yy * 2 + ll, pl.ds(pl.multiple_of(core * rows + lo, 16), n)]

    own_bel = {}
    for p in range(n_p):
        for t in range(KS):
            own_bel[p, t] = pltpu.make_async_copy(
                bel_ref.at[pl.ds(starts[p], PIECE_ROWS[p]), pl.ds(t * TILE, TILE)],
                g_refs[p].at[zh * KS + t], bel_sem.at[p, t],
            )
            own_bel[p, t].start()
    mine = block(y, zl)
    own_alp = pltpu.make_async_copy(alp_ref, mine, loc_sem.at[0])
    own_alp.start()
    own_obs = pltpu.make_async_copy(obs_hbm, obs_ref, loc_sem.at[1])
    own_tiles = pltpu.make_async_copy(tiles_hbm, tiles_ref, loc_sem.at[2])

    nt = tact_ref.shape[1]
    act_l = jnp.broadcast_to(tact_ref[...].astype(F32), (nt, nt))
    dst_l = jnp.broadcast_to((tdst_ref[...] & (cols // TILE - 1)).astype(F32), (nt, nt))
    src_s = jnp.transpose(jnp.broadcast_to(tsrc_ref[...].astype(F32), (nt, nt)))
    act_s, dst_s = jnp.transpose(act_l), jnp.transpose(dst_l)
    sub = lax.broadcasted_iota(jnp.int32, (nt, nt), 0)
    lan = lax.broadcasted_iota(jnp.int32, (nt, nt), 1)
    one = jnp.ones((nt, nt), F32)
    nil = jnp.zeros((nt, nt), F32)
    rank = jnp.sum(jnp.where((act_l == act_s) & (lan < sub), one, nil), axis=1, keepdims=True)
    lane = lax.broadcasted_iota(jnp.int32, (nt, 128), 1).astype(F32)
    by_rank = jnp.where(rank == lane, 1.0, 0.0).astype(BF16)
    by_act = jnp.where(act_s[:, :1] == lane, src_s[:, :1], 0.0).astype(BF16)
    table = lax.dot_general(by_rank, by_act, (((0,), (0,)), ((), ())), preferred_element_type=F32)
    tabs_ref[0] = table[:KS].astype(jnp.int32)
    rank_row = jnp.sum(jnp.where((act_l == act_s) & (sub < lan), one, nil), axis=0, keepdims=True)
    same_row = jnp.sum(jnp.where((dst_l == dst_s) & (sub < lan), one, nil), axis=0, keepdims=True)
    place = jnp.where((dst_l < dst_s) | ((dst_l == dst_s) & (lan < sub)), one, nil)
    place = jnp.sum(place, axis=1, keepdims=True)
    by_place = jnp.where(place == lane, 1.0, 0.0).astype(BF16)
    row8 = lax.broadcasted_iota(jnp.int32, (8, nt), 0)
    facts = jnp.where(row8 == 0, act_l[:8], jnp.where(row8 == 1, jnp.broadcast_to(rank_row, (8, nt)), 0.0))
    facts = jnp.where(row8 == 2, lan[:8].astype(F32), facts)
    facts = jnp.where(row8 == 3, jnp.broadcast_to(jnp.minimum(same_row, 1.0), (8, nt)), facts)
    slot_tab = jnp.dot(facts.astype(BF16), by_place, preferred_element_type=F32)
    upto = jnp.sum(jnp.where(dst_s[:, :1] <= lane, 1.0, 0.0), axis=0, keepdims=True)
    here = jnp.sum(jnp.where(dst_s[:, :1] == lane, 1.0, 0.0), axis=0, keepdims=True)
    last = jnp.broadcast_to(jnp.maximum(upto - 1.0, 0.0), (8, 128))
    some = jnp.broadcast_to(jnp.minimum(here, 1.0), (8, 128))
    row8 = lax.broadcasted_iota(jnp.int32, (8, 128), 0)
    slot_tab = jnp.where(row8 == 4, last, jnp.where(row8 == 5, some, slot_tab))
    slot_ref[...] = slot_tab.astype(jnp.int32)

    act_col = jnp.transpose(jnp.broadcast_to(act_ref[...].astype(F32), (rows, rows)))
    for p in range(n_p):
        m_refs[p][...] = jnp.zeros_like(m_refs[p])
    for a in range(ACT):
        hit = jnp.where(act_col == float(a), 1.0, 0.0).astype(BF16)
        for c in range(TILE // rows):
            part = slice(c * rows, (c + 1) * rows)
            full_ref[a, :, part] = hit
            for p in range(n_p):
                m_refs[p][a * NX, :, part] = hit[starts[p] : starts[p] + PIECE_ROWS[p]]

    for c in own_bel.values():
        c.wait()
    all_here(near)

    sends = []

    def go(c):
        c.start()
        sends.append(c)
        return c

    def own_send(p, d):
        part = g_refs[p].at[pl.ds(zh * KS, KS)]
        return remote(part, part, z_send.at[d, p], z_recv.at[d, p], z_dev[d])

    def forward(p, d):
        origin = (zh + 3) % NZ if d == 0 else (zh + 1) % NZ
        part = g_refs[p].at[pl.ds(origin * KS + d * kh, kh)]
        return remote(part, part, f_send.at[d, p], f_recv.at[d, p], z_dev[d])

    own = {}
    for p in range(2):
        for d in range(2):
            own[p, d] = go(own_send(p, d))

    tab_copies = [
        go(remote(tabs_ref.at[0], tabs_ref.at[j], tab_send.at[j], tab_recv.at[j], x_dev[j - 1]))
        for j in range(1, NX)
    ]

    n_b = [0]

    def b_copy(part, dev):
        i = n_b[0]
        n_b[0] += 1
        return go(remote(part, part, b_send.at[i], b_recv.at[i], dev))

    own_alp.wait()
    own_tiles.start()
    own_obs.start()
    b_up = b_copy(mine, y_dev[0])
    b_down = b_copy(mine, y_dev[1])
    b_sib = [b_copy(mine, sib_dev)]
    p_sib = [[], []]
    half = rows // 2

    def ring_forward(ll, lo, n, up, down, sib):
        up.wait_recv()
        one = b_copy(block((y + 3) % 4, ll, lo, n // 2), y_dev[0])
        down.wait_recv()
        two = b_copy(block((y + 1) % 4, ll, lo + n // 2, n // 2), y_dev[1])
        for yy in ((y + 3) % 4, (y + 1) % 4):
            sib.append(b_copy(block(yy, ll, lo, n), sib_dev))
        return one, two

    def ring_end(ll, lo, n, stage, sib):
        stage[0].wait_recv()
        stage[1].wait_recv()
        sib.append(b_copy(block((y + 2) % 4, ll, lo, n), sib_dev))

    for c in tab_copies:
        c.wait_recv()
    to_smem = pltpu.make_async_copy(tabs_ref, smem_ref, loc_sem.at[3])
    to_smem.start()
    slots_to_smem = pltpu.make_async_copy(slot_ref, slot_smem, loc_sem.at[4])
    slots_to_smem.start()
    to_smem.wait()
    slots_to_smem.wait()

    def pick(j, p, into):
        part = pl.ds(starts[p], PIECE_ROWS[p])

        def one(k, carry):
            acc = None
            for a in range(ACT):
                src = smem_ref[(NX - j) % NX, k, a]
                tile = g_refs[p][src & (NZ * KS - 1)]
                away = ((src >> 5) + NX - x) & (NX - 1)
                m = m_refs[p][a * NX + away]
                acc = tile * m if acc is None else acc + tile * m
            into[k, part] = acc
            return carry

        lax.fori_loop(0, KS, one, 0)

    fwd = {}
    x_copies = []

    def along_x(p):
        part = pl.ds(starts[p], PIECE_ROWS[p])
        fwd[p, 0].wait_recv()
        fwd[p, 1].wait_recv()
        for j in (2, 1, 3):
            pick(j, p, pick_ref.at[j - 1])
            x_copies.append(go(remote(
                pick_ref.at[j - 1, :, part], land_ref.at[j, :, part],
                x_send.at[j, p], x_recv.at[j, p], x_dev[j - 1],
            )))
        pick(0, p, land_ref.at[0])

    partner = 1 - zl
    for p in range(n_p):
        for d in range(2):
            own[p, d].wait_recv()
            fwd[p, d] = go(forward(p, d))
        if p + 2 < n_p:
            for d in range(2):
                own[p + 2, d] = go(own_send(p + 2, d))
        if p == n_p - 1:
            pair = [b_copy(block(y, zl, c * half, half), pair_dev) for c in range(2)]
        if p == 1:
            stage = ring_forward(zl, 0, rows, b_up, b_down, b_sib)
        if p == 2:
            ring_end(zl, 0, rows, stage, b_sib)
        if p:
            along_x(p - 1)
    along_x(n_p - 1)

    def partner_out(c):
        pair[c].wait_recv()
        part = block(y, partner, c * half, half)
        out = b_copy(part, y_dev[0]), b_copy(part, y_dev[1])
        p_sib[c].append(b_copy(part, sib_dev))
        return out

    for c in x_copies:
        c.wait_recv()

    def merge(k, carry):
        r_ref[k] = (land_ref[0, k] + land_ref[1, k]) + (land_ref[2, k] + land_ref[3, k])
        return carry

    lax.fori_loop(0, KS, merge, 0)
    round0 = partner_out(0)

    own_tiles.wait()
    own_obs.wait()
    seg_ref[0] = jnp.zeros_like(seg_ref[0])

    def eight(o, carry):
        for e in range(8):
            i = o * 8 + e
            left = r_ref[slot_smem[1, i] & (KS - 1)] * full_ref[slot_smem[0, i] & (ACT - 1)]
            part = jnp.dot(left, tiles_ref[slot_smem[2, i] & (nt - 1)], preferred_element_type=F32)
            seg_ref[i + 1] = seg_ref[i] * slot_smem[3, i].astype(F32) + part
        return carry

    lax.fori_loop(0, nt // 8, eight, 0)

    code = act_ref[...] * OBS + seen_ref[...]
    codes = lax.broadcasted_iota(jnp.int32, (ACT * OBS, rows), 0)
    hot = jnp.where(codes == code, 1.0, 0.0).astype(BF16)
    total = jnp.zeros((rows, 1), F32)
    for d in range(cols // TILE):
        part = pl.ds(d * TILE, TILE)
        seen = lax.dot_general(
            hot, obs_ref[:, part], (((0,), (0,)), ((), ())), preferred_element_type=F32
        )
        reached = seg_ref[(slot_smem[4, d] & (nt - 1)) + 1] * slot_smem[5, d].astype(F32)
        un = reached * seen
        unnorm_ref[:, part] = un
        u_ref[:, part] = un.astype(BF16)
        total = total + jnp.sum(un, axis=1, keepdims=True)
    tot_ref[...] = jnp.transpose(jnp.broadcast_to(total, (rows, rows)))[:8]

    tot_x = [
        go(remote(tot_ref, totx_ref.at[j], t_send.at[0, j], t_recv.at[0, j], x_dev[j - 1]))
        for j in range(1, NX)
    ]

    quarter = rows // NX
    cx = {}

    def score(n, yy, ll):
        c_ref[n] = lax.dot_general(
            u_ref[...], b_ref[yy * 2 + ll], (((1,), (1,)), ((), ())), preferred_element_type=F32
        )
        for j in (2, 1, 3):
            xx = (x + j) % NX
            cx[n, j] = go(remote(
                c_ref.at[n, pl.ds(pl.multiple_of(xx * quarter, quarter), quarter)], xr_ref.at[j, n],
                cx_send.at[n, j], cx_recv.at[n, j], x_dev[j - 1],
            ))

    each = quarter // NZ
    per = NB // GROUPS
    cz = {}

    def along_z(h):
        for n in range(h * per, (h + 1) * per):
            for j in range(1, NX):
                cx[n, j].wait_recv()
            own_part = c_ref[n, pl.ds(pl.multiple_of(x * quarter, quarter), quarter)]
            d_ref[n] = (own_part + xr_ref[1, n]) + (xr_ref[2, n] + xr_ref[3, n])
        part = pl.ds(h * per, per)
        for j in (2, 1, 3):
            zz = (zh + j) % NZ
            cz[h, j] = go(remote(
                d_ref.at[part, pl.ds(pl.multiple_of(zz * each, each), each)], zr_ref.at[j, part],
                cz_send.at[h, j], cz_recv.at[h, j], z_all[j - 1],
            ))

    for c in b_sib:
        c.wait_recv()
    for i in range(4):
        score(i, (y + i) % 4, zl)
    round1 = partner_out(1)
    stage0 = ring_forward(partner, 0, half, *round0, p_sib[0])
    for c in tot_x:
        c.wait_recv()
    totx_ref[0] = (tot_ref[...] + totx_ref[1]) + (totx_ref[2] + totx_ref[3])
    tot_z = [
        go(remote(totx_ref.at[0], totz_ref.at[j], t_send.at[1, j], t_recv.at[1, j], z_all[j - 1]))
        for j in range(1, NZ)
    ]
    along_z(0)
    stage1 = ring_forward(partner, half, half, *round1, p_sib[1])
    along_z(1)
    ring_end(partner, 0, half, stage0, p_sib[0])
    for c in range(2):
        p_sib[c][0].wait_recv()
    score(4, y, partner)
    for c in range(2):
        p_sib[c][1].wait_recv()
        p_sib[c][2].wait_recv()
    score(5, (y + 1) % 4, partner)
    score(6, (y + 3) % 4, partner)
    ring_end(partner, half, half, stage1, p_sib[1])
    for c in range(2):
        p_sib[c][3].wait_recv()
    score(7, (y + 2) % 4, partner)

    for c in tot_z:
        c.wait_recv()
    all_tot = (totx_ref[0] + totz_ref[1]) + (totz_ref[2] + totz_ref[3])
    tcol_ref[...] = jnp.transpose(jnp.broadcast_to(all_tot[0:1], (rows, rows)))

    def norm(i, carry):
        part = pl.ds(pl.multiple_of(i * rows, rows), rows)
        new_ref[:, part] = ((scale * unnorm_ref[:, part]) / tcol_ref[...]).astype(BF16)
        return carry

    lax.fori_loop(0, cols // rows, norm, 0)
    along_z(2)
    along_z(3)

    best = None
    for h in range(GROUPS):
        for j in range(1, NZ):
            cz[h, j].wait_recv()
        for n in range(h * per, (h + 1) * per):
            own_part = d_ref[n, pl.ds(pl.multiple_of(zh * each, each), each)]
            full = (own_part + zr_ref[1, n]) + (zr_ref[2, n] + zr_ref[3, n])
            best = full if best is None else jnp.maximum(best, full)
    top = jnp.max(best, axis=1, keepdims=True)
    div = tcol_ref[pl.ds(pl.multiple_of(s * each, each), each)]
    val_ref[...] = jnp.broadcast_to(top, div.shape) / div
    for c in sends:
        c.wait_send()


def per_device(
    beliefs, tiles, tile_src, tile_dst, tile_action, obs_prob, action_index, obs_index, alphas
):
    n_vec = lax.axis_size("vec")
    n_state = lax.axis_size("state")
    rows, cols = beliefs.shape
    nt = tile_src.shape[0]
    wide = n_vec * alphas.shape[0] // NB
    quarter = rows // NX
    n_p = len(PIECE_ROWS)
    dma = pltpu.SemaphoreType.DMA
    vmem = pl.BlockSpec(memory_space=pltpu.VMEM)
    hbm = pl.BlockSpec(memory_space=pl.ANY)
    new_belief, value = pl.pallas_call(
        functools.partial(expand_kernel, float(cols * n_state)),
        out_shape=(
            jax.ShapeDtypeStruct((rows, cols), BF16),
            jax.ShapeDtypeStruct((rows // n_state, rows), F32),
        ),
        in_specs=[vmem, vmem, vmem, vmem, vmem, hbm, hbm, hbm, hbm],
        out_specs=(vmem, vmem),
        scratch_shapes=[
            *[pltpu.VMEM((NZ * KS, r, TILE), BF16) for r in PIECE_ROWS],
            *[pltpu.VMEM((ACT * NX, r, TILE), BF16) for r in PIECE_ROWS],
            pltpu.VMEM((NX - 1, KS, rows, TILE), BF16),
            pltpu.VMEM((NX, KS, rows, TILE), BF16),
            pltpu.VMEM((KS, rows, TILE), BF16),
            pltpu.VMEM((ACT, rows, TILE), BF16),
            pltpu.VMEM((NX, 8, 128), jnp.int32),
            pltpu.VMEM((8, 128), jnp.int32),
            pltpu.SMEM((NX, 8, 128), jnp.int32),
            pltpu.SMEM((8, 128), jnp.int32),
            pltpu.VMEM(tiles.shape, BF16),
            pltpu.VMEM((ACT * OBS, cols), BF16),
            pltpu.VMEM((nt + 1, rows, TILE), F32),
            pltpu.VMEM((rows, cols), F32),
            pltpu.VMEM((rows, cols), BF16),
            pltpu.VMEM((NB, wide, cols), BF16),
            pltpu.VMEM((NB, rows, wide), F32),
            pltpu.VMEM((NX, NB, quarter, wide), F32),
            pltpu.VMEM((NB, quarter, wide), F32),
            pltpu.VMEM((NZ, NB, quarter // NZ, wide), F32),
            pltpu.VMEM((8, rows), F32),
            pltpu.VMEM((NX, 8, rows), F32),
            pltpu.VMEM((NZ, 8, rows), F32),
            pltpu.VMEM((rows, rows), F32),
            dma((n_p, KS)), dma((5,)), dma((NX,)), dma((NX,)),
            dma((2, n_p)), dma((2, n_p)), dma((2, n_p)), dma((2, n_p)),
            dma((NX, n_p)), dma((NX, n_p)), dma((32,)), dma((32,)),
            dma((NB, NX)), dma((NB, NX)), dma((GROUPS, NZ)), dma((GROUPS, NZ)),
            dma((2, NX)), dma((2, NX)),
        ],
        compiler_params=pltpu.CompilerParams(
            collective_id=0, has_side_effects=True, vmem_limit_bytes=BIG
        ),
    )(
        tile_src[None, :], tile_action[None, :], tile_dst[None, :], action_index[None, :],
        obs_index[None, :], beliefs, alphas, tiles, obs_prob.reshape(ACT * OBS, cols),
    )
    return new_belief, value[:, 0]


def solution(mesh):
    placed = (
        P("vec", "state"),
        P("state", None, None),
        P("state"),
        P("state"),
        P("state"),
        P(None, None, "state"),
        P("vec"),
        P("vec"),
        P("vec", "state"),
    )
    return jax.shard_map(
        per_device,
        mesh=mesh,
        in_specs=placed,
        out_specs=(P("vec", "state"), P(("vec", "state"))),
        check_vma=False,
    )
```
